256 devices in a mesh: row: 8 (over z), col: 32 (over x, y, core).
Axes of the slice: x: 4, y: 4, z: 8, core: 2. Of those that a mesh axis runs over, the one named last changes fastest.
Arguments:
- h_values: float32 [8, 512, 4096], P('row', 'col'), as said below
- h_places: int32 [8, 512], P('row', 'col'), may hold values from 0 to 15, as said below
- h_counts: int32 [8, 32], P('row', 'col'), may hold values from 0 to 16, as said below
- p_values: float32 [8, 512, 4096], P('row', 'col'), as said below
- p_places: int32 [8, 512], P('row', 'col'), may hold values from 0 to 15, as said below
- p_counts: int32 [8, 32], P('row', 'col'), may hold values from 0 to 16, as said below
- s_values: float32 [8, 512, 4096], P('row', 'col'), as said below
- s_places: int32 [8, 512], P('row', 'col'), may hold values from 0 to 15, as said below
- s_counts: int32 [8, 32], P('row', 'col'), may hold values from 0 to 16, as said below
- x_places: int32 [8, 512], P('row', 'col'), may hold values from 0 to 15, as said below
- x_counts: int32 [8, 32], P('row', 'col'), may hold values from 0 to 16, as said below
Outputs:
- gradient: float32 [8, 512, 4096], P('row', 'col')
The draws below stay inside these ranges and needn't reach their ends.
Inputs may be any that keep to these rules, and one draw needn't show every extreme that they name: `h_places`: in each tile the 16 entries are a permutation of the tile's positions; the first count entries are the present blocks. Every pattern is symmetric, holds every block whose block row and block column lie in the same row panel, and every block (i, j) whose cyclic block distance min(|i - j|, 64 - |i - j|) is 2 or less or exactly 32. `p_places`: as for h_places. `s_places`: as for h_places. `x_places`: as for h_places. `h_counts`: every tile whose block columns lie in its own row panel is full. `p_counts`: as for h_counts. `s_counts`: as for h_counts. `x_counts`: as for h_counts. `h_values`: the assembled H is symmetric. `p_values`: the assembled P is symmetric. `s_values`: the assembled S is symmetric.
All inputs are finite; a program needn't handle non-finite values.
Results may differ from the reference program's by a relative error of at most 0.000088.
Values sent between devices are 32-bit elements; how exact they have to be, the bound alone decides.
A program may use at most 64 MiB of HBM per device.

```python
import jax
import jax.numpy as jnp
from jax import lax

BS = 64
TC = 2
NB = 64
TR = 8
CAP = 16
ORDER = 4096


def pattern(key, salt_value):
    base = jax.random.fold_in(key, salt_value)
    first_key, second_key, third_key = jax.random.split(base, 3)
    panel_rows = NB // TR
    panel_cols = NB // TC
    random_codes = jax.random.randint(first_key, (NB, NB), 0, 4)
    symmetric = jnp.minimum(random_codes, random_codes.T)
    block_ids = jnp.arange(NB)
    distance_raw = jnp.abs(block_ids[:, None] - block_ids[None, :])
    distance = jnp.minimum(distance_raw, NB - distance_raw)
    offsets = jax.random.randint(third_key, (3,), 3, NB // 2 + 1)
    on_far = jnp.any(distance[..., None] == offsets[None, None, :], axis=-1) & (symmetric > 0)
    half_box = distance == NB // 2
    same_panel = block_ids[:, None] // TR == block_ids[None, :] // TR
    present = (same_panel | (distance <= 2) | on_far | half_box).astype(jnp.int32)
    tile_flags = present.reshape(panel_rows, TR, panel_cols, TC).transpose(0, 2, 1, 3).reshape(panel_rows, panel_cols, CAP)
    shuffle = jax.random.randint(second_key, (panel_rows, panel_cols, CAP), 0, 2 ** 20)
    ranking_keys = (1 - tile_flags) * 2 ** 25 + shuffle * CAP + jnp.arange(CAP)
    places = jnp.argsort(ranking_keys, axis=-1, stable=True).astype(jnp.int32)
    counts = jnp.sum(tile_flags, axis=-1).astype(jnp.int32)
    return (places, counts)


def matrix_values(key, salt_value):
    places, counts = pattern(key, salt_value)
    panel_rows = NB // TR
    panel_cols = NB // TC
    value_key = jax.random.fold_in(key, salt_value + 100)
    raw_entries = jax.random.normal(value_key, (ORDER, ORDER), jnp.float32)
    factor = (0.5 / (BS * (TR + 5))) ** (1.0 / 3.0)
    full_matrix = (raw_entries + raw_entries.T) * factor
    blocks = full_matrix.reshape(panel_rows, TR, BS, panel_cols, TC, BS).transpose(0, 3, 1, 4, 2, 5)
    blocks = blocks.reshape(panel_rows, panel_cols, CAP, BS * BS)
    picked = jnp.take_along_axis(blocks, places[..., None], axis=2)
    return picked.reshape(panel_rows, panel_cols * CAP, BS * BS)


def list_of(key, salt_value):
    places, counts = pattern(key, salt_value)
    return places.reshape(NB // TR, NB // TC * CAP)


def count_of(key, salt_value):
    places, counts = pattern(key, salt_value)
    return counts


def draw_h_values(key, part):
    return matrix_values(key, 11)


def draw_h_places(key, part):
    return list_of(key, 11)


def draw_h_counts(key, part):
    return count_of(key, 11)


def draw_p_values(key, part):
    return matrix_values(key, 23)


def draw_p_places(key, part):
    return list_of(key, 23)


def draw_p_counts(key, part):
    return count_of(key, 23)


def draw_s_values(key, part):
    return matrix_values(key, 37)


def draw_s_places(key, part):
    return list_of(key, 37)


def draw_s_counts(key, part):
    return count_of(key, 37)


def draw_x_places(key, part):
    return list_of(key, 41)


def draw_x_counts(key, part):
    return count_of(key, 41)


def setup_inputs(seed: int = 0) -> dict:
    streams_of = jax.random.split(jax.random.key(seed), 12)
    h_values = draw_h_values(jax.random.fold_in(streams_of[11], 71), 0)
    h_places = draw_h_places(jax.random.fold_in(streams_of[11], 71), 0)
    h_counts = draw_h_counts(jax.random.fold_in(streams_of[11], 71), 0)
    p_values = draw_p_values(jax.random.fold_in(streams_of[11], 71), 0)
    p_places = draw_p_places(jax.random.fold_in(streams_of[11], 71), 0)
    p_counts = draw_p_counts(jax.random.fold_in(streams_of[11], 71), 0)
    s_values = draw_s_values(jax.random.fold_in(streams_of[11], 71), 0)
    s_places = draw_s_places(jax.random.fold_in(streams_of[11], 71), 0)
    s_counts = draw_s_counts(jax.random.fold_in(streams_of[11], 71), 0)
    x_places = draw_x_places(jax.random.fold_in(streams_of[11], 71), 0)
    x_counts = draw_x_counts(jax.random.fold_in(streams_of[11], 71), 0)
    return dict(h_values=h_values, h_places=h_places, h_counts=h_counts, p_values=p_values, p_places=p_places, p_counts=p_counts, s_values=s_values, s_places=s_places, s_counts=s_counts, x_places=x_places, x_counts=x_counts)


def assemble(values, places, counts):
    panel_rows = NB // TR
    panel_cols = NB // TC
    blocks_in = values.reshape(panel_rows, panel_cols, CAP, BS * BS).astype(jnp.float32)
    positions = places.reshape(panel_rows, panel_cols, CAP)
    slot_ids = jnp.arange(CAP, dtype=jnp.int32)
    matches = (positions[..., None] == slot_ids) & (slot_ids[:, None] < counts[..., None, None])
    tiles = jnp.einsum("rcsp,rcsv->rcpv", matches.astype(jnp.float32), blocks_in, precision=lax.Precision.HIGHEST)
    tiles = tiles.reshape(panel_rows, panel_cols, TR, TC, BS, BS)
    return tiles.transpose(0, 2, 4, 1, 3, 5).reshape(ORDER, ORDER)


def pattern_mask(places, counts):
    panel_rows = NB // TR
    panel_cols = NB // TC
    positions = places.reshape(panel_rows, panel_cols, CAP)
    slot_ids = jnp.arange(CAP, dtype=jnp.int32)
    matches = (positions[..., None] == slot_ids) & (slot_ids[:, None] < counts[..., None, None])
    present = jnp.sum(matches.astype(jnp.float32), axis=2)
    present = present.reshape(panel_rows, panel_cols, TR, TC).transpose(0, 2, 1, 3).reshape(NB, NB)
    return jnp.broadcast_to(present[:, None, :, None], (NB, BS, NB, BS)).reshape(ORDER, ORDER)


def to_slots(matrix, places, counts):
    panel_rows = NB // TR
    panel_cols = NB // TC
    blocks = matrix.reshape(panel_rows, TR, BS, panel_cols, TC, BS).transpose(0, 3, 1, 4, 2, 5)
    blocks = blocks.reshape(panel_rows, panel_cols, CAP, BS * BS)
    positions = places.reshape(panel_rows, panel_cols, CAP).astype(jnp.int32)
    picked = jnp.take_along_axis(blocks, positions[..., None], axis=2)
    slot_ids = jnp.arange(CAP, dtype=jnp.int32)
    used = (slot_ids[None, None, :] < counts[..., None]).astype(matrix.dtype)
    picked = picked * used[..., None]
    return picked.reshape(panel_rows, panel_cols * CAP, BS * BS)


def reference(h_values, h_places, h_counts, p_values, p_places, p_counts, s_values, s_places, s_counts, x_places, x_counts):
    kohn_sham = assemble(h_values, h_places, h_counts)
    density = assemble(p_values, p_places, p_counts)
    intersection = assemble(s_values, s_places, s_counts)
    allowed = pattern_mask(x_places, x_counts)
    first = allowed * jnp.dot(kohn_sham, density, precision=lax.Precision.HIGHEST)
    second = allowed * jnp.dot(first, intersection, precision=lax.Precision.HIGHEST)
    return to_slots(second + second.T, x_places, x_counts)
```

```python
import jax
import jax.numpy as jnp
from jax import lax
from jax.experimental import pallas as pl
from jax.experimental.pallas import tpu as pltpu
from jax.sharding import PartitionSpec as P

MESH = pl.DeviceIdType.MESH
F32 = jnp.float32
BF16 = jnp.bfloat16
BS = 64
CAP = 16
TILE = 512
WIDTH = 128
HALF = 256
QUARTER = 128
NCOPY = 160


def split(value):
    high = value.astype(BF16)
    return high, (value - high.astype(F32)).astype(BF16)


def kernel(
    index_ref, h_ref, p_ref, s_ref, out_ref,
    hv, pv, sv, hb, yb, pt, st, pb, sb, rhs, acc, part, xt, xs, tr, zt, bl,
    send_sem, recv_sem, local_sem,
):
    z = lax.axis_index("row")
    col = lax.axis_index("col")
    q = lax.rem(col, 2)
    y = lax.rem(col // 2, 4)
    x = col // 8
    lane = lax.broadcasted_iota(jnp.int32, (32, WIDTH), 1)
    low = lane < BS

    def device(dz, dx, dy):
        return (
            lax.rem(z + dz, 8),
            lax.rem(x + dx, 4) * 8 + lax.rem(y + dy, 4) * 2 + q,
        )

    partner = (z, col + 1 - 2 * q)
    mirror_row = col // 4

    def mirror(g):
        return (mirror_row, 4 * z + g)

    diagonal = mirror_row == z
    own_place = lax.rem(col, 4)

    barrier = pltpu.get_barrier_semaphore()
    for target in (
        device(0, 0, 1), device(0, 0, 3), device(0, 1, 0), device(0, 3, 0),
        device(1, 0, 0), device(7, 0, 0), partner,
    ):
        pl.semaphore_signal(barrier, inc=1, device_id=target, device_id_type=MESH)
    for g in range(4):
        @pl.when(jnp.logical_or(mirror_row != z, own_place != g))
        def _(g=g):
            pl.semaphore_signal(barrier, inc=1, device_id=mirror(g), device_id_type=MESH)

    used = {}

    def copy(name, src, dst, target):
        if name not in used:
            used[name] = len(used)
        n = used[name]
        return pltpu.make_async_remote_copy(
            src_ref=src, dst_ref=dst, send_sem=send_sem.at[n], recv_sem=recv_sem.at[n],
            device_id=target, device_id_type=MESH,
        )

    started, gifts = [], []

    def send(name, src, dst, target, kept=None):
        made = copy(name, src, dst, target)
        made.start()
        (started if kept is None else kept).append(made)

    def arrived(name, dst):
        copy(name, dst, dst, partner).wait_recv()

    def place_rows(values, base, dst, index):
        @pl.loop(0, 8)
        def _(i):
            a = values[index_ref[base + 2 * i]]
            b = values[index_ref[base + 2 * i + 1]]
            top = jnp.where(low, a, pltpu.roll(b, BS, 1))
            bottom = jnp.where(low, pltpu.roll(a, BS, 1), b)
            start = pl.multiple_of(i * BS, BS)
            dst[index, pl.ds(start, 32), :] = top
            dst[index, pl.ds(start + 32, 32), :] = bottom

    def place_natural(values, base, dst):
        for i in range(8):
            a = values[index_ref[base + 2 * i]]
            b = values[index_ref[base + 2 * i + 1]]
            even = jnp.where(low, a, pltpu.roll(b, BS, 1))
            odd = jnp.where(low, pltpu.roll(a, BS, 1), b)
            g = i // 2
            view = dst.at[g % 2, g // 2]
            view[pl.ds((i % 2) * BS, 32, 2), :] = even
            view[pl.ds((i % 2) * BS + 1, 32, 2), :] = odd

    for source, values in ((h_ref, hv), (p_ref, pv), (s_ref, sv)):
        values[pl.ds(0, CAP)] = source[...]
        values[CAP] = jnp.zeros((32, WIDTH), F32)
    here = x * 4 + y
    place_rows(hv, 0, hb, here)
    place_natural(pv, CAP, pt)
    place_natural(sv, 2 * CAP, st)

    pl.semaphore_wait(barrier, jnp.where(diagonal, 10, 11))

    def tile_at(first, a, b):
        dy, dx = (a, b) if first == 1 else (b, a)
        return lax.rem(x + dx, 4) * 4 + lax.rem(y + dy, 4)

    def step(first, stage, by):
        along_y = (first == 1) == (stage == 1)
        return device(0, 0, by) if along_y else device(0, by, 0)

    def whole(buf, half, a, b):
        return buf.at[tile_at(1 - half, a, b), pl.ds(half * HALF, HALF)]

    def quarter(buf, half, a, b, k):
        return buf.at[tile_at(1 - half, a, b), pl.ds(half * HALF + k * QUARTER, QUARTER)]

    def first_out(tag, buf, half):
        src = whole(buf, half, 0, 0)
        send((tag, half, "s1", 1), src, src, step(1 - half, 1, 1))
        send((tag, half, "s1", 3), src, src, step(1 - half, 1, 3))

    def second_out(tag, buf, half, a):
        src = whole(buf, half, a, 0)
        send((tag, half, "s2", a, 1), src, src, step(1 - half, 2, 1))
        send((tag, half, "s2", a, 3), src, src, step(1 - half, 2, 3))

    def first_in(tag, buf, half):
        for by, a, k in ((1, 3, 0), (3, 1, 1)):
            arrived((tag, half, "s1", by), whole(buf, half, a, 0))
            src = quarter(buf, half, a, 0, k)
            send((tag, half, "f1", by), src, src, step(1 - half, 1, by))
            second_out(tag, buf, half, a)

    def first_far(tag, buf, half):
        for by, k in ((1, 0), (3, 1)):
            arrived((tag, half, "f1", by), quarter(buf, half, 2, 0, k))
        second_out(tag, buf, half, 2)

    def second_in(tag, buf, half, a):
        for by, b, k in ((1, 3, 0), (3, 1, 1)):
            arrived((tag, half, "s2", a, by), whole(buf, half, a, b))
            src = quarter(buf, half, a, b, k)
            send((tag, half, "f2", a, by), src, src, step(1 - half, 2, by))

    def second_far(tag, buf, half, a):
        for by, k in ((1, 0), (3, 1)):
            arrived((tag, half, "f2", a, by), quarter(buf, half, a, 2, k))

    def ring_start(tag, own, buf):
        keep = pltpu.make_async_copy(own.at[q], buf.at[z, q], local_sem.at[0 if tag == "p" else 1])
        keep.start()
        send((tag, "mate"), own.at[1 - q], buf.at[z, q], partner)
        for by in (1, 7):
            send((tag, "own", by, 1), own.at[q], buf.at[z, q], device(by, 0, 0))
        return keep

    def ring_mate(tag, buf):
        arrived((tag, "mate"), buf.at[z, 1 - q])
        src = buf.at[z, 1 - q]
        for by in (1, 7):
            send((tag, "other", by, 1), src, src, device(by, 0, 0))

    def ring_in(tag, buf, d):
        for kind, core in (("own", q), ("other", 1 - q)):
            for by in (1, 7):
                away = lax.rem(z + (8 - by) * d, 8)
                if d < 4:
                    arrived((tag, kind, by, d), buf.at[away, core])
                if d < 3:
                    src = buf.at[away, core]
                    send((tag, kind, by, d + 1), src, src, device(by, 0, 0))
                elif d == 3:
                    src = buf.at[away, core, 0 if by == 1 else 1]
                    send((tag, kind, by, 4), src, src, device(by, 0, 0))
                else:
                    arrived((tag, kind, by, 4), buf.at[away, core, 0 if by == 1 else 1])

    def weights(buf, away):
        for g in range(2):
            wide = jnp.concatenate([buf[away, 0, g], buf[away, 1, g]], axis=1)
            high, rest = split(wide)
            t = 2 * away + g
            rhs[t, pl.ds(0, 128), :] = high
            rhs[t, pl.ds(128, 128), :] = high
            rhs[t, pl.ds(256, 128), :] = rest

    def weights_at(buf, d):
        @pl.loop(0, 2 if d < 4 else 1)
        def _(k):
            weights(buf, lax.rem(z + jnp.where(k == 0, d, 8 - d), 8))

    def product(buf, half):
        rows = pl.ds(half * HALF, HALF)
        acc[0, rows, :] = jnp.zeros((HALF, WIDTH), F32)
        acc[1, rows, :] = jnp.zeros((HALF, WIDTH), F32)

        @pl.loop(0, 16)
        def _(t):
            high, rest = split(buf[t, rows, :])
            left = jnp.concatenate([high, rest, high], axis=1)
            term = jnp.dot(left, rhs[t], preferred_element_type=F32)
            acc[0, rows, :] += term[:, :WIDTH]
            acc[1, rows, :] += term[:, WIDTH:]

    def give(tag, half):
        rows = pl.ds(half * HALF, HALF)
        send((tag, half), acc.at[1 - q, rows], part.at[0 if tag == "dy" else 1, rows], partner,
             gifts if tag == "dy" else None)

    first_out("h", hb, 0)
    first_out("h", hb, 1)
    keep_p = ring_start("p", pt, pb)
    second_out("h", hb, 0, 0)
    second_out("h", hb, 1, 0)
    ring_mate("p", pb)
    keep_s = ring_start("s", st, sb)
    first_in("h", hb, 0)
    first_in("h", hb, 1)
    keep_p.wait()

    @pl.loop(0, 1)
    def _(k):
        weights(pb, z)

    ring_in("p", pb, 1)
    weights_at(pb, 1)
    first_far("h", hb, 0)
    first_far("h", hb, 1)
    second_in("h", hb, 0, 0)
    second_in("h", hb, 1, 0)
    ring_in("p", pb, 2)
    weights_at(pb, 2)
    for a in (3, 1):
        second_in("h", hb, 0, a)
        second_in("h", hb, 1, a)
    ring_in("p", pb, 3)
    weights_at(pb, 3)
    second_in("h", hb, 0, 2)
    second_in("h", hb, 1, 2)
    ring_mate("s", sb)
    ring_in("s", sb, 1)
    for a in (0, 3, 1, 2):
        second_far("h", hb, 0, a)
        second_far("h", hb, 1, a)
    ring_in("p", pb, 4)
    weights_at(pb, 4)
    product(hb, 0)
    give("dy", 0)
    product(hb, 1)
    give("dy", 1)

    for half in range(2):
        rows = pl.ds(half * HALF, HALF)
        arrived(("dy", half), part.at[0, rows])
        for i in range(4 * half, 4 * half + 4):
            wide = lax.broadcasted_iota(jnp.int32, (BS, WIDTH), 1)
            kept = jnp.where(wide < BS, index_ref[4 * CAP + 2 * i], index_ref[4 * CAP + 2 * i + 1]) > 0
            strip = pl.ds(i * BS, BS)
            yb[here, strip, :] = jnp.where(kept, acc[q, strip, :] + part[0, strip, :], 0.0)
        first_out("y", yb, half)
        second_out("y", yb, half, 0)

    keep_s.wait()

    @pl.loop(0, 1)
    def _(k):
        weights(sb, z)

    weights_at(sb, 1)
    ring_in("s", sb, 2)
    weights_at(sb, 2)
    first_in("y", yb, 0)
    first_in("y", yb, 1)
    first_far("y", yb, 0)
    first_far("y", yb, 1)
    second_in("y", yb, 0, 0)
    second_in("y", yb, 1, 0)
    ring_in("s", sb, 3)
    weights_at(sb, 3)
    for a in (3, 1):
        second_in("y", yb, 0, a)
        second_in("y", yb, 1, a)
    second_in("y", yb, 0, 2)
    second_in("y", yb, 1, 2)
    ring_in("s", sb, 4)
    weights_at(sb, 4)
    for a in (0, 3, 1, 2):
        second_far("y", yb, 0, a)
        second_far("y", yb, 1, a)
    for made in gifts:
        made.wait_send()
    product(yb, 0)
    give("dx", 0)
    product(yb, 1)
    give("dx", 1)

    def chunk(g):
        return pltpu.make_async_remote_copy(
            src_ref=xs.at[g], dst_ref=tr.at[own_place], send_sem=send_sem.at[NCOPY + g],
            recv_sem=recv_sem.at[NCOPY + own_place], device_id=mirror(g), device_id_type=MESH,
        )

    def leaves(g):
        return jnp.logical_or(mirror_row != z, own_place != g)

    for half in range(2):
        arrived(("dx", half), part.at[1, pl.ds(half * HALF, HALF)])
        for g in (2 * half, 2 * half + 1):
            for k in range(2):
                base = g * QUARTER + k * BS
                for odd in range(2):
                    strip = pl.ds(base + 32 * odd, 32)
                    value = acc[q, strip, :] + part[1, strip, :]
                    xt[strip, :] = value
                    xs[g, pl.ds(k * BS + odd, 32, 2), :] = value

            @pl.when(leaves(g))
            def _(g=g):
                chunk(g).start()

            @pl.when(jnp.logical_not(leaves(g)))
            def _(g=g):
                stay = pltpu.make_async_copy(xs.at[g], tr.at[g], local_sem.at[2])
                stay.start()
                stay.wait()

    bl[CAP] = jnp.zeros((32, WIDTH), F32)
    for g in range(4):
        @pl.when(leaves(g))
        def _(g=g):
            pltpu.make_async_remote_copy(
                src_ref=xs.at[g], dst_ref=tr.at[g], send_sem=send_sem.at[NCOPY + g],
                recv_sem=recv_sem.at[NCOPY + g], device_id=mirror(g), device_id_type=MESH,
            ).wait_recv()

        zt[...] = tr[g].T
        for k in range(2):
            i = 2 * g + k
            top = xt[pl.ds(i * BS, 32), :] + zt[pl.ds(k * BS, 32, 2), :]
            bottom = xt[pl.ds(i * BS + 32, 32), :] + zt[pl.ds(k * BS + 1, 32, 2), :]
            bl[2 * i] = jnp.where(low, top, pltpu.roll(bottom, BS, 1))
            bl[2 * i + 1] = jnp.where(low, pltpu.roll(top, BS, 1), bottom)

    @pl.loop(0, CAP)
    def _(slot):
        out_ref[slot] = bl[index_ref[3 * CAP + slot]]

    for g in range(4):
        @pl.when(leaves(g))
        def _(g=g):
            chunk(g).wait_send()

    for made in started:
        made.wait_send()


def shards(
    h_values, h_places, h_counts, p_values, p_places, p_counts,
    s_values, s_places, s_counts, x_places, x_counts,
):
    slots = lax.iota(jnp.int32, CAP)

    def slot_of(places, counts):
        match = (places[0][:, None] == slots[None, :]) & (slots[:, None] < counts[0, 0])
        return jnp.min(jnp.where(match, slots[:, None], CAP), axis=0)

    index = jnp.concatenate([
        slot_of(h_places, h_counts), slot_of(p_places, p_counts), slot_of(s_places, s_counts),
        jnp.where(slots < x_counts[0, 0], x_places[0], CAP),
        (slot_of(x_places, x_counts) < CAP).astype(jnp.int32),
    ])

    def blocks(values):
        return values.reshape(CAP, 32, WIDTH)

    vmem = pl.BlockSpec(memory_space=pltpu.VMEM)
    smem = pl.BlockSpec(memory_space=pltpu.SMEM)
    out = pl.pallas_call(
        kernel,
        out_shape=jax.ShapeDtypeStruct((CAP, 32, WIDTH), F32),
        in_specs=[smem, vmem, vmem, vmem],
        out_specs=vmem,
        scratch_shapes=[
            pltpu.VMEM((CAP + 1, 32, WIDTH), F32),
            pltpu.VMEM((CAP + 1, 32, WIDTH), F32),
            pltpu.VMEM((CAP + 1, 32, WIDTH), F32),
            pltpu.VMEM((16, TILE, WIDTH), F32),
            pltpu.VMEM((16, TILE, WIDTH), F32),
            pltpu.VMEM((2, 2, 128, WIDTH), F32),
            pltpu.VMEM((2, 2, 128, WIDTH), F32),
            pltpu.VMEM((8, 2, 2, 128, WIDTH), F32),
            pltpu.VMEM((8, 2, 2, 128, WIDTH), F32),
            pltpu.VMEM((16, 384, 2 * WIDTH), BF16),
            pltpu.VMEM((2, TILE, WIDTH), F32),
            pltpu.VMEM((2, TILE, WIDTH), F32),
            pltpu.VMEM((TILE, WIDTH), F32),
            pltpu.VMEM((4, 128, WIDTH), F32),
            pltpu.VMEM((4, 128, WIDTH), F32),
            pltpu.VMEM((128, WIDTH), F32),
            pltpu.VMEM((CAP + 1, 32, WIDTH), F32),
            pltpu.SemaphoreType.DMA((NCOPY + 4,)),
            pltpu.SemaphoreType.DMA((NCOPY + 4,)),
            pltpu.SemaphoreType.DMA((3,)),
        ],
        compiler_params=pltpu.CompilerParams(
            collective_id=0, has_side_effects=True, vmem_limit_bytes=48 * 1024 * 1024
        ),
    )(index, blocks(h_values), blocks(p_values), blocks(s_values))
    return out.reshape(1, CAP, BS * BS)


def solution(mesh):
    tile = P("row", "col", None)
    flat = P("row", "col")
    in_specs = (tile, flat, flat) * 3 + (flat, flat)
    return jax.shard_map(shards, mesh=mesh, in_specs=in_specs, out_specs=tile, check_vma=False)
```

```python
import jax
import jax.numpy as jnp
from jax import lax
from jax.experimental import pallas as pl
from jax.experimental.pallas import tpu as pltpu
from jax.sharding import PartitionSpec as P

MESH = pl.DeviceIdType.MESH
F32 = jnp.float32
BF16 = jnp.bfloat16
BS = 64
CAP = 16
TILE = 512
WIDTH = 128
HALF = 256
QUARTER = 128
NCOPY = 208


def split(value):
    high = value.astype(BF16)
    return high, (value - high.astype(F32)).astype(BF16)


def kernel(
    hp_ref, hc_ref, pp_ref, pc_ref, sp_ref, sc_ref, xp_ref, xc_ref, h_ref, p_ref, s_ref, out_ref,
    hp, hc, pp, pc, sp, sc, xp, xc, index_ref, raw, hv, pv, sv, hb, yb, pt, st, pb, sb, rhs_p, rhs_s, acc, part, xt, xs, tr, zt, bl,
    im, send_sem, recv_sem, local_sem, load_sem,
):
    loads = [
        pltpu.make_async_copy(src, dst, load_sem.at[n])
        for n, (src, dst) in enumerate((
            (hp_ref, hp), (hc_ref, hc), (pp_ref, pp), (pc_ref, pc), (sp_ref, sp), (sc_ref, sc),
            (xp_ref, xp), (xc_ref, xc), (h_ref, raw.at[0]), (p_ref, raw.at[1]), (s_ref, raw.at[2]),
        ))
    ]
    for load in loads:
        load.start()
    z = lax.axis_index("row")
    col = lax.axis_index("col")
    q = lax.rem(col, 2)
    y = lax.rem(col // 2, 4)
    x = col // 8
    lane = lax.broadcasted_iota(jnp.int32, (32, WIDTH), 1)
    low = lane < BS

    def device(dz, dx, dy):
        return (
            lax.rem(z + dz, 8),
            lax.rem(x + dx, 4) * 8 + lax.rem(y + dy, 4) * 2 + q,
        )

    partner = (z, col + 1 - 2 * q)
    mirror_row = col // 4

    own_place = lax.rem(col, 4)

    panel = mirror_row
    middle = (z, 4 * lax.rem(z + panel, 8) + own_place)
    giver = (z, 4 * lax.rem(panel - z + 8, 8) + own_place)

    def final(g):
        return (lax.rem(panel - z + 8, 8), 4 * z + g)

    def relay(k):
        return (panel, 4 * lax.rem(z + panel, 8) + k)

    def other(device_id):
        return jnp.logical_or(device_id[0] != z, device_id[1] != col)

    barrier = pltpu.get_barrier_semaphore()
    for target in (
        device(0, 0, 1), device(0, 0, 3), device(0, 1, 0), device(0, 3, 0),
        device(1, 0, 0), device(7, 0, 0), partner,
    ):
        pl.semaphore_signal(barrier, inc=1, device_id=target, device_id_type=MESH)
    for target in (giver, *(relay(k) for k in range(4))):
        @pl.when(other(target))
        def _(target=target):
            pl.semaphore_signal(barrier, inc=1, device_id=target, device_id_type=MESH)
    expected = 7 + jnp.where(other(middle), 1, 0)
    for g in range(4):
        expected = expected + jnp.where(other(final(g)), 1, 0)

    used = {}

    def copy(name, src, dst, target):
        if name not in used:
            used[name] = len(used)
        n = used[name]
        return pltpu.make_async_remote_copy(
            src_ref=src, dst_ref=dst, send_sem=send_sem.at[n], recv_sem=recv_sem.at[n],
            device_id=target, device_id_type=MESH,
        )

    started, gifts = [], []

    def send(name, src, dst, target, kept=None):
        made = copy(name, src, dst, target)
        made.start()
        (started if kept is None else kept).append(made)

    def arrived(name, dst):
        copy(name, dst, dst, partner).wait_recv()

    def place_rows(values, base, dst, index):
        @pl.loop(0, 8)
        def _(i):
            a = values[index_ref[base + 2 * i]]
            b = values[index_ref[base + 2 * i + 1]]
            top = jnp.where(low, a, pltpu.roll(b, BS, 1))
            bottom = jnp.where(low, pltpu.roll(a, BS, 1), b)
            start = pl.multiple_of(i * BS, BS)
            dst[index, pl.ds(start, 32), :] = top
            dst[index, pl.ds(start + 32, 32), :] = bottom

    def place_natural(values, base, dst):
        for i in range(8):
            a = values[index_ref[base + 2 * i]]
            b = values[index_ref[base + 2 * i + 1]]
            even = jnp.where(low, a, pltpu.roll(b, BS, 1))
            odd = jnp.where(low, pltpu.roll(a, BS, 1), b)
            g = i // 2
            view = dst.at[g % 2, g // 2]
            view[pl.ds((i % 2) * BS, 32, 2), :] = even
            view[pl.ds((i % 2) * BS + 1, 32, 2), :] = odd

    for load in loads:
        load.wait()
    for m, (places, counts) in enumerate(((hp, hc), (pp, pc), (sp, sc), (xp, xc))):
        count = counts[0, 0]

        @pl.loop(0, CAP)
        def _(place, m=m, places=places, count=count):
            slot = CAP
            for k in range(CAP):
                slot = jnp.where(jnp.logical_and(places[0, k] == place, k < count), k, slot)
            index_ref[m * CAP + place] = slot

    @pl.loop(0, CAP)
    def _(slot):
        index_ref[4 * CAP + slot] = jnp.where(slot < xc[0, 0], xp[0, slot], CAP)

    for m, values in enumerate((hv, pv, sv)):
        values[pl.ds(0, CAP)] = raw[m, 0].reshape(CAP, 32, WIDTH)
        values[CAP] = jnp.zeros((32, WIDTH), F32)
    here = x * 4 + y
    place_rows(hv, 0, hb, here)
    place_natural(pv, CAP, pt)
    place_natural(sv, 2 * CAP, st)

    pl.semaphore_wait(barrier, expected)

    def tile_at(first, a, b):
        dy, dx = (a, b) if first == 1 else (b, a)
        return lax.rem(x + dx, 4) * 4 + lax.rem(y + dy, 4)

    def step(first, stage, by):
        along_y = (first == 1) == (stage == 1)
        return device(0, 0, by) if along_y else device(0, by, 0)

    def whole(buf, part, side, a, b):
        return buf.at[tile_at(1 - side, a, b), pl.ds(part * HALF + side * QUARTER, QUARTER)]

    def piece(buf, part, side, a, b, k):
        start = part * HALF + side * QUARTER + k * BS
        return buf.at[tile_at(1 - side, a, b), pl.ds(start, BS)]

    def second_out(tag, buf, part, side, a):
        src = whole(buf, part, side, a, 0)
        for by in (1, 3):
            send((tag, part, side, "s2", a, by), src, src, step(1 - side, 2, by))

    def out(tag, buf, part):
        for side in range(2):
            src = whole(buf, part, side, 0, 0)
            for by in (1, 3):
                send((tag, part, side, "s1", by), src, src, step(1 - side, 1, by))
        for side in range(2):
            second_out(tag, buf, part, side, 0)

    def first_in(tag, buf, part):
        for by, a, k in ((1, 3, 0), (3, 1, 1)):
            for side in range(2):
                arrived((tag, part, side, "s1", by), whole(buf, part, side, a, 0))
                src = piece(buf, part, side, a, 0, k)
                send((tag, part, side, "f1", by), src, src, step(1 - side, 1, by))
                second_out(tag, buf, part, side, a)

    def first_far(tag, buf, part):
        for side in range(2):
            for by, k in ((1, 0), (3, 1)):
                arrived((tag, part, side, "f1", by), piece(buf, part, side, 2, 0, k))
            second_out(tag, buf, part, side, 2)

    def second_in(tag, buf, part, a):
        for by, b, k in ((1, 3, 0), (3, 1, 1)):
            for side in range(2):
                arrived((tag, part, side, "s2", a, by), whole(buf, part, side, a, b))
                src = piece(buf, part, side, a, b, k)
                send((tag, part, side, "f2", a, by), src, src, step(1 - side, 2, by))

    def second_far(tag, buf, part):
        for a in (0, 3, 1, 2):
            for side in range(2):
                for by, k in ((1, 0), (3, 1)):
                    arrived((tag, part, side, "f2", a, by), piece(buf, part, side, a, 2, k))

    def ring_start(tag, own, buf):
        keep = pltpu.make_async_copy(own.at[q], buf.at[z, q], local_sem.at[0 if tag == "p" else 1])
        keep.start()
        send((tag, "mate"), own.at[1 - q], buf.at[z, q], partner)
        for by in (1, 7):
            send((tag, "own", by, 1), own.at[q], buf.at[z, q], device(by, 0, 0))
        return keep

    def ring_mate(tag, buf):
        arrived((tag, "mate"), buf.at[z, 1 - q])
        src = buf.at[z, 1 - q]
        for by in (1, 7):
            send((tag, "other", by, 1), src, src, device(by, 0, 0))

    def ring_in(tag, buf, d):
        for kind, core in (("own", q), ("other", 1 - q)):
            for by in (1, 7):
                away = lax.rem(z + (8 - by) * d, 8)
                if d < 4:
                    arrived((tag, kind, by, d), buf.at[away, core])
                if d < 3:
                    src = buf.at[away, core]
                    send((tag, kind, by, d + 1), src, src, device(by, 0, 0))
                elif d == 3:
                    src = buf.at[away, core, 0 if by == 1 else 1]
                    send((tag, kind, by, 4), src, src, device(by, 0, 0))
                else:
                    arrived((tag, kind, by, 4), buf.at[away, core, 0 if by == 1 else 1])

    def weights(buf, rhs, away):
        for g in range(2):
            wide = jnp.concatenate([buf[away, 0, g], buf[away, 1, g]], axis=1)
            high, rest = split(wide)
            t = 2 * away + g
            rhs[t, pl.ds(0, 128), :] = high
            rhs[t, pl.ds(128, 128), :] = high
            rhs[t, pl.ds(256, 128), :] = rest

    def weights_at(buf, rhs, d):
        @pl.loop(0, 2 if d < 4 else 1)
        def _(k):
            weights(buf, rhs, lax.rem(z + jnp.where(k == 0, d, 8 - d), 8))

    def product(buf, rhs, half):
        rows = pl.ds(half * HALF, HALF)
        acc[0, rows, :] = jnp.zeros((HALF, WIDTH), F32)
        acc[1, rows, :] = jnp.zeros((HALF, WIDTH), F32)

        @pl.loop(0, 2)
        def _(t):
            parts = []
            for k in range(8):
                high, rest = split(buf[8 * t + k, rows, :])
                parts += [high, rest, high]
            term = jnp.dot(
                jnp.concatenate(parts, axis=1),
                rhs[pl.ds(8 * t, 8)].reshape(8 * 384, 2 * WIDTH),
                preferred_element_type=F32,
            )
            acc[0, rows, :] += term[:, :WIDTH]
            acc[1, rows, :] += term[:, WIDTH:]

    def give(tag, half):
        rows = pl.ds(half * HALF, HALF)
        send((tag, half), acc.at[1 - q, rows], part.at[0 if tag == "dy" else 1, rows], partner,
             gifts if tag == "dy" else None)

    def masked(half):
        rows = pl.ds(half * HALF, HALF)
        arrived(("dy", half), part.at[0, rows])
        wide = lax.broadcasted_iota(jnp.int32, (BS, WIDTH), 1)
        for i in range(4 * half, 4 * half + 4):
            kept = jnp.where(wide < BS, index_ref[3 * CAP + 2 * i], index_ref[3 * CAP + 2 * i + 1]) < CAP
            strip = pl.ds(i * BS, BS)
            yb[here, strip, :] = jnp.where(kept, acc[q, strip, :] + part[0, strip, :], 0.0)
        out("y", yb, half)

    out("h", hb, 0)
    keep_p = ring_start("p", pt, pb)
    ring_mate("p", pb)
    first_in("h", hb, 0)
    out("h", hb, 1)
    keep_p.wait()
    weights(pb, rhs_p, z)
    second_in("h", hb, 0, 0)
    ring_in("p", pb, 1)
    first_far("h", hb, 0)
    first_in("h", hb, 1)
    weights_at(pb, rhs_p, 1)
    second_in("h", hb, 0, 3)
    second_in("h", hb, 0, 1)
    second_in("h", hb, 1, 0)
    ring_in("p", pb, 2)
    first_far("h", hb, 1)
    weights_at(pb, rhs_p, 2)
    second_in("h", hb, 0, 2)
    second_far("h", hb, 0)
    second_in("h", hb, 1, 3)
    second_in("h", hb, 1, 1)
    ring_in("p", pb, 3)
    keep_s = ring_start("s", st, sb)
    ring_mate("s", sb)
    weights_at(pb, rhs_p, 3)
    second_in("h", hb, 1, 2)
    ring_in("p", pb, 4)
    weights_at(pb, rhs_p, 4)
    product(hb, rhs_p, 0)
    give("dy", 0)
    second_far("h", hb, 1)
    product(hb, rhs_p, 1)
    give("dy", 1)

    masked(0)
    keep_s.wait()
    weights(sb, rhs_s, z)
    first_in("y", yb, 0)
    masked(1)
    ring_in("s", sb, 1)
    weights_at(sb, rhs_s, 1)
    second_in("y", yb, 0, 0)
    first_far("y", yb, 0)
    first_in("y", yb, 1)
    ring_in("s", sb, 2)
    weights_at(sb, rhs_s, 2)
    second_in("y", yb, 0, 3)
    second_in("y", yb, 0, 1)
    second_in("y", yb, 1, 0)
    first_far("y", yb, 1)
    ring_in("s", sb, 3)
    weights_at(sb, rhs_s, 3)
    second_in("y", yb, 0, 2)
    second_in("y", yb, 1, 3)
    second_in("y", yb, 1, 1)
    second_far("y", yb, 0)
    ring_in("s", sb, 4)
    weights_at(sb, rhs_s, 4)
    gifts[0].wait_send()
    product(yb, rhs_s, 0)
    give("dx", 0)
    second_in("y", yb, 1, 2)
    gifts[1].wait_send()

    def to_middle(g):
        return pltpu.make_async_remote_copy(
            src_ref=xs.at[g], dst_ref=im.at[g], send_sem=send_sem.at[NCOPY + g],
            recv_sem=recv_sem.at[NCOPY + g], device_id=middle, device_id_type=MESH,
        )

    def onward(g):
        return pltpu.make_async_remote_copy(
            src_ref=im.at[g], dst_ref=tr.at[own_place], send_sem=send_sem.at[NCOPY + 4 + g],
            recv_sem=recv_sem.at[NCOPY + 4 + own_place], device_id=final(g), device_id_type=MESH,
        )

    def stay(src, dst):
        copied = pltpu.make_async_copy(src, dst, local_sem.at[2])
        copied.start()
        copied.wait()

    def either(away, there, here_):
        pl.when(away)(there)
        pl.when(jnp.logical_not(away))(here_)

    def chunks_out(half):
        arrived(("dx", half), part.at[1, pl.ds(half * HALF, HALF)])
        for g in (2 * half, 2 * half + 1):
            for k in range(2):
                base = g * QUARTER + k * BS
                for odd in range(2):
                    strip = pl.ds(base + 32 * odd, 32)
                    value = acc[q, strip, :] + part[1, strip, :]
                    xt[strip, :] = value
                    xs[g, pl.ds(k * BS + odd, 32, 2), :] = value
            either(
                other(middle),
                lambda g=g: to_middle(g).start(),
                lambda g=g: stay(xs.at[g], im.at[g]),
            )

    def chunks_on(half):
        for g in (2 * half, 2 * half + 1):
            @pl.when(other(giver))
            def _(g=g):
                to_middle(g).wait_recv()

            either(
                other(final(g)),
                lambda g=g: onward(g).start(),
                lambda g=g: stay(im.at[g], tr.at[g]),
            )

    chunks_out(0)
    second_far("y", yb, 1)
    product(yb, rhs_s, 1)
    give("dx", 1)
    chunks_on(0)
    chunks_out(1)
    chunks_on(1)

    bl[CAP] = jnp.zeros((32, WIDTH), F32)
    for g in range(4):
        @pl.when(other(relay(g)))
        def _(g=g):
            pltpu.make_async_remote_copy(
                src_ref=tr.at[g], dst_ref=tr.at[g], send_sem=send_sem.at[NCOPY + 4 + g],
                recv_sem=recv_sem.at[NCOPY + 4 + g], device_id=partner, device_id_type=MESH,
            ).wait_recv()

        zt[...] = tr[g].T
        for k in range(2):
            i = 2 * g + k
            top = xt[pl.ds(i * BS, 32), :] + zt[pl.ds(k * BS, 32, 2), :]
            bottom = xt[pl.ds(i * BS + 32, 32), :] + zt[pl.ds(k * BS + 1, 32, 2), :]
            bl[2 * i] = jnp.where(low, top, pltpu.roll(bottom, BS, 1))
            bl[2 * i + 1] = jnp.where(low, pltpu.roll(top, BS, 1), bottom)

    @pl.loop(0, CAP)
    def _(slot):
        out_ref[slot] = bl[index_ref[4 * CAP + slot]]

    for g in range(4):
        @pl.when(other(middle))
        def _(g=g):
            to_middle(g).wait_send()

        @pl.when(other(final(g)))
        def _(g=g):
            onward(g).wait_send()

    for made in started:
        made.wait_send()


def shards(
    h_values, h_places, h_counts, p_values, p_places, p_counts,
    s_values, s_places, s_counts, x_places, x_counts,
):
    vmem = pl.BlockSpec(memory_space=pltpu.VMEM)
    anywhere = pl.BlockSpec(memory_space=pl.ANY)
    out = pl.pallas_call(
        kernel,
        out_shape=jax.ShapeDtypeStruct((CAP, 32, WIDTH), F32),
        in_specs=[anywhere] * 11,
        out_specs=vmem,
        scratch_shapes=[
            pltpu.SMEM((1, CAP), jnp.int32), pltpu.SMEM((1, 1), jnp.int32),
            pltpu.SMEM((1, CAP), jnp.int32), pltpu.SMEM((1, 1), jnp.int32),
            pltpu.SMEM((1, CAP), jnp.int32), pltpu.SMEM((1, 1), jnp.int32),
            pltpu.SMEM((1, CAP), jnp.int32), pltpu.SMEM((1, 1), jnp.int32),
            pltpu.SMEM((5 * CAP,), jnp.int32),
            pltpu.VMEM((3, 1, CAP, BS * BS), F32),
            pltpu.VMEM((CAP + 1, 32, WIDTH), F32),
            pltpu.VMEM((CAP + 1, 32, WIDTH), F32),
            pltpu.VMEM((CAP + 1, 32, WIDTH), F32),
            pltpu.VMEM((16, TILE, WIDTH), F32),
            pltpu.VMEM((16, TILE, WIDTH), F32),
            pltpu.VMEM((2, 2, 128, WIDTH), F32),
            pltpu.VMEM((2, 2, 128, WIDTH), F32),
            pltpu.VMEM((8, 2, 2, 128, WIDTH), F32),
            pltpu.VMEM((8, 2, 2, 128, WIDTH), F32),
            pltpu.VMEM((16, 384, 2 * WIDTH), BF16),
            pltpu.VMEM((16, 384, 2 * WIDTH), BF16),
            pltpu.VMEM((2, TILE, WIDTH), F32),
            pltpu.VMEM((2, TILE, WIDTH), F32),
            pltpu.VMEM((TILE, WIDTH), F32),
            pltpu.VMEM((4, 128, WIDTH), F32),
            pltpu.VMEM((4, 128, WIDTH), F32),
            pltpu.VMEM((128, WIDTH), F32),
            pltpu.VMEM((CAP + 1, 32, WIDTH), F32),
            pltpu.VMEM((4, 128, WIDTH), F32),
            pltpu.SemaphoreType.DMA((NCOPY + 8,)),
            pltpu.SemaphoreType.DMA((NCOPY + 8,)),
            pltpu.SemaphoreType.DMA((3,)),
            pltpu.SemaphoreType.DMA((11,)),
        ],
        compiler_params=pltpu.CompilerParams(
            collective_id=0, has_side_effects=True, vmem_limit_bytes=48 * 1024 * 1024
        ),
    )(
        h_places, h_counts, p_places, p_counts, s_places, s_counts, x_places, x_counts,
        h_values, p_values, s_values,
    )
    return out.reshape(1, CAP, BS * BS)


def solution(mesh):
    tile = P("row", "col", None)
    flat = P("row", "col")
    in_specs = (tile, flat, flat) * 3 + (flat, flat)
    return jax.shard_map(shards, mesh=mesh, in_specs=in_specs, out_specs=tile, check_vma=False)
```

```python
import jax
import jax.numpy as jnp
from jax import lax
from jax.experimental import pallas as pl
from jax.experimental.pallas import tpu as pltpu
from jax.sharding import PartitionSpec as P

MESH = pl.DeviceIdType.MESH
F32 = jnp.float32
BF16 = jnp.bfloat16
BS = 64
CAP = 16
TILE = 512
WIDTH = 128
HALF = 256
QUARTER = 128
NCOPY = 198
POOL = 48


def split(value):
    high = value.astype(BF16)
    return high, (value - high.astype(F32)).astype(BF16)


def kernel(
    hp_ref, hc_ref, pp_ref, pc_ref, sp_ref, sc_ref, xp_ref, xc_ref, h_ref, p_ref, s_ref, out_ref,
    hp, hc, pp, pc, sp, sc, xp, xc, index_ref, raw, hv, pv, sv, hb, yb, pt, st, pb, sb, rhs_p, rhs_s, acc, part, xt, xs, tr, zt, bl,
    im, send_sem, recv_sem, local_sem, load_sem,
):
    loads = [
        pltpu.make_async_copy(src, dst, load_sem.at[n])
        for n, (src, dst) in enumerate((
            (hp_ref, hp), (hc_ref, hc), (pp_ref, pp), (pc_ref, pc), (sp_ref, sp), (sc_ref, sc),
            (xp_ref, xp), (xc_ref, xc), (h_ref, raw.at[0]), (p_ref, raw.at[1]), (s_ref, raw.at[2]),
        ))
    ]
    for load in loads:
        load.start()
    z = lax.axis_index("row")
    col = lax.axis_index("col")
    q = lax.rem(col, 2)
    y = lax.rem(col // 2, 4)
    x = col // 8
    lane = lax.broadcasted_iota(jnp.int32, (32, WIDTH), 1)
    low = lane < BS

    def device(dz, dx, dy):
        return (
            lax.rem(z + dz, 8),
            lax.rem(x + dx, 4) * 8 + lax.rem(y + dy, 4) * 2 + q,
        )

    partner = (z, col + 1 - 2 * q)
    mirror_row = col // 4

    own_place = lax.rem(col, 4)

    panel = mirror_row
    middle = (z, 4 * lax.rem(z + panel, 8) + own_place)
    giver = (z, 4 * lax.rem(panel - z + 8, 8) + own_place)

    def final(g):
        return (lax.rem(panel - z + 8, 8), 4 * z + g)

    def relay(k):
        return (panel, 4 * lax.rem(z + panel, 8) + k)

    def other(device_id):
        return jnp.logical_or(device_id[0] != z, device_id[1] != col)

    barrier = pltpu.get_barrier_semaphore()
    for target in (
        device(0, 0, 1), device(0, 0, 3), device(0, 1, 0), device(0, 3, 0),
        device(1, 0, 0), device(7, 0, 0), partner,
    ):
        pl.semaphore_signal(barrier, inc=1, device_id=target, device_id_type=MESH)
    for target in (giver, *(relay(k) for k in range(4))):
        @pl.when(other(target))
        def _(target=target):
            pl.semaphore_signal(barrier, inc=1, device_id=target, device_id_type=MESH)
    expected = 7 + jnp.where(other(middle), 1, 0)
    for g in range(4):
        expected = expected + jnp.where(other(final(g)), 1, 0)

    used, started, gifts = {}, [], []

    def copy(name, src, dst, target, sent=0):
        if name not in used:
            used[name] = len(used)
        return pltpu.make_async_remote_copy(
            src_ref=src, dst_ref=dst, send_sem=send_sem.at[sent], recv_sem=recv_sem.at[used[name]],
            device_id=target, device_id_type=MESH,
        )

    def send(name, src, dst, target, kept=None):
        if kept is None:
            if len(started) >= POOL:
                started[-POOL].wait_send()
            made = copy(name, src, dst, target, len(started) % POOL)
            started.append(made)
        else:
            made = copy(name, src, dst, target, POOL + len(kept))
            kept.append(made)
        made.start()

    def arrived(name, dst):
        copy(name, dst, dst, partner).wait_recv()

    def place_rows(values, base, dst, index):
        @pl.loop(0, 8)
        def _(i):
            a = values[index_ref[base + 2 * i]]
            b = values[index_ref[base + 2 * i + 1]]
            top = jnp.where(low, a, pltpu.roll(b, BS, 1))
            bottom = jnp.where(low, pltpu.roll(a, BS, 1), b)
            start = pl.multiple_of(i * BS, BS)
            dst[index, pl.ds(start, 32), :] = top
            dst[index, pl.ds(start + 32, 32), :] = bottom

    def place_natural(values, base, dst):
        for i in range(8):
            a = values[index_ref[base + 2 * i]]
            b = values[index_ref[base + 2 * i + 1]]
            even = jnp.where(low, a, pltpu.roll(b, BS, 1))
            odd = jnp.where(low, pltpu.roll(a, BS, 1), b)
            g = i // 2
            view = dst.at[g % 2, g // 2]
            view[pl.ds((i % 2) * BS, 32, 2), :] = even
            view[pl.ds((i % 2) * BS + 1, 32, 2), :] = odd

    for load in loads:
        load.wait()
    for m, (places, counts) in enumerate(((hp, hc), (pp, pc), (sp, sc), (xp, xc))):
        count = counts[0, 0]

        @pl.loop(0, CAP)
        def _(place, m=m, places=places, count=count):
            slot = CAP
            for k in range(CAP):
                slot = jnp.where(jnp.logical_and(places[0, k] == place, k < count), k, slot)
            index_ref[m * CAP + place] = slot

    @pl.loop(0, CAP)
    def _(slot):
        index_ref[4 * CAP + slot] = jnp.where(slot < xc[0, 0], xp[0, slot], CAP)

    for m, values in enumerate((hv, pv, sv)):
        values[pl.ds(0, CAP)] = raw[m, 0].reshape(CAP, 32, WIDTH)
        values[CAP] = jnp.zeros((32, WIDTH), F32)
    here = x * 4 + y
    place_rows(hv, 0, hb, here)
    place_natural(pv, CAP, pt)
    place_natural(sv, 2 * CAP, st)

    pl.semaphore_wait(barrier, expected)

    def tile_at(first, a, b):
        dy, dx = (a, b) if first == 1 else (b, a)
        return lax.rem(x + dx, 4) * 4 + lax.rem(y + dy, 4)

    def step(first, stage, by):
        along_y = (first == 1) == (stage == 1)
        return device(0, 0, by) if along_y else device(0, by, 0)

    def whole(buf, part, side, a, b):
        return buf.at[tile_at(1 - side, a, b), pl.ds(part * HALF + side * QUARTER, QUARTER)]

    def piece(buf, part, side, a, b, k):
        start = part * HALF + side * QUARTER + k * BS
        return buf.at[tile_at(1 - side, a, b), pl.ds(start, BS)]

    def second_out(tag, buf, part, side, a):
        src = whole(buf, part, side, a, 0)
        for by in (1, 3):
            send((tag, part, side, "s2", a, by), src, src, step(1 - side, 2, by))

    def out(tag, buf, part):
        for side in range(2):
            src = whole(buf, part, side, 0, 0)
            for by in (1, 3):
                send((tag, part, side, "s1", by), src, src, step(1 - side, 1, by))
        for side in range(2):
            second_out(tag, buf, part, side, 0)

    def first_in(tag, buf, part):
        for by, a, k in ((1, 3, 0), (3, 1, 1)):
            for side in range(2):
                arrived((tag, part, side, "s1", by), whole(buf, part, side, a, 0))
                src = piece(buf, part, side, a, 0, k)
                send((tag, part, side, "f1", by), src, src, step(1 - side, 1, by))
                second_out(tag, buf, part, side, a)

    def first_far(tag, buf, part):
        for side in range(2):
            for by, k in ((1, 0), (3, 1)):
                arrived((tag, part, side, "f1", by), piece(buf, part, side, 2, 0, k))
            second_out(tag, buf, part, side, 2)

    def second_in(tag, buf, part, a):
        for by, b, k in ((1, 3, 0), (3, 1, 1)):
            for side in range(2):
                arrived((tag, part, side, "s2", a, by), whole(buf, part, side, a, b))
                src = piece(buf, part, side, a, b, k)
                send((tag, part, side, "f2", a, by), src, src, step(1 - side, 2, by))

    def second_far(tag, buf, part):
        for a in (0, 3, 1, 2):
            for side in range(2):
                for by, k in ((1, 0), (3, 1)):
                    arrived((tag, part, side, "f2", a, by), piece(buf, part, side, a, 2, k))

    def ring_start(tag, own, buf):
        keep = pltpu.make_async_copy(own.at[q], buf.at[z, q], local_sem.at[0 if tag == "p" else 1])
        keep.start()
        send((tag, "mate"), own.at[1 - q], buf.at[z, q], partner)
        for by in (1, 7):
            send((tag, "own", by, 1), own.at[q], buf.at[z, q], device(by, 0, 0))
        return keep

    def ring_mate(tag, buf):
        arrived((tag, "mate"), buf.at[z, 1 - q])
        src = buf.at[z, 1 - q]
        for by in (1, 7):
            send((tag, "other", by, 1), src, src, device(by, 0, 0))

    def ring_in(tag, buf, d):
        for kind, core in (("own", q), ("other", 1 - q)):
            for by in (1, 7):
                away = lax.rem(z + (8 - by) * d, 8)
                if d < 4:
                    arrived((tag, kind, by, d), buf.at[away, core])
                if d < 3:
                    src = buf.at[away, core]
                    send((tag, kind, by, d + 1), src, src, device(by, 0, 0))
                elif d == 3:
                    src = buf.at[away, core, 0 if by == 1 else 1]
                    send((tag, kind, by, 4), src, src, device(by, 0, 0))
                else:
                    arrived((tag, kind, by, 4), buf.at[away, core, 0 if by == 1 else 1])

    def weights(buf, rhs, away):
        for g in range(2):
            wide = jnp.concatenate([buf[away, 0, g], buf[away, 1, g]], axis=1)
            high, rest = split(wide)
            t = 2 * away + g
            rhs[t, pl.ds(0, 128), :] = high
            rhs[t, pl.ds(128, 128), :] = high
            rhs[t, pl.ds(256, 128), :] = rest

    def weights_at(buf, rhs, d):
        @pl.loop(0, 2 if d < 4 else 1)
        def _(k):
            weights(buf, rhs, lax.rem(z + jnp.where(k == 0, d, 8 - d), 8))

    def product(buf, rhs, half):
        rows = pl.ds(half * HALF, HALF)
        acc[0, rows, :] = jnp.zeros((HALF, WIDTH), F32)
        acc[1, rows, :] = jnp.zeros((HALF, WIDTH), F32)

        @pl.loop(0, 2)
        def _(t):
            parts = []
            for k in range(8):
                high, rest = split(buf[8 * t + k, rows, :])
                parts += [high, rest, high]
            term = jnp.dot(
                jnp.concatenate(parts, axis=1),
                rhs[pl.ds(8 * t, 8)].reshape(8 * 384, 2 * WIDTH),
                preferred_element_type=F32,
            )
            acc[0, rows, :] += term[:, :WIDTH]
            acc[1, rows, :] += term[:, WIDTH:]

    def give(tag, half):
        rows = pl.ds(half * HALF, HALF)
        send((tag, half), acc.at[1 - q, rows], part.at[0 if tag == "dy" else 1, rows], partner,
             gifts if tag == "dy" else None)

    def masked(half):
        rows = pl.ds(half * HALF, HALF)
        arrived(("dy", half), part.at[0, rows])
        wide = lax.broadcasted_iota(jnp.int32, (BS, WIDTH), 1)
        for i in range(4 * half, 4 * half + 4):
            kept = jnp.where(wide < BS, index_ref[3 * CAP + 2 * i], index_ref[3 * CAP + 2 * i + 1]) < CAP
            strip = pl.ds(i * BS, BS)
            yb[here, strip, :] = jnp.where(kept, acc[q, strip, :] + part[0, strip, :], 0.0)
        out("y", yb, half)

    out("h", hb, 0)
    keep_p = ring_start("p", pt, pb)
    ring_mate("p", pb)
    first_in("h", hb, 0)
    out("h", hb, 1)
    keep_p.wait()
    weights(pb, rhs_p, z)
    second_in("h", hb, 0, 0)
    ring_in("p", pb, 1)
    first_far("h", hb, 0)
    first_in("h", hb, 1)
    weights_at(pb, rhs_p, 1)
    second_in("h", hb, 0, 3)
    second_in("h", hb, 0, 1)
    second_in("h", hb, 1, 0)
    ring_in("p", pb, 2)
    first_far("h", hb, 1)
    weights_at(pb, rhs_p, 2)
    second_in("h", hb, 0, 2)
    second_far("h", hb, 0)
    second_in("h", hb, 1, 3)
    second_in("h", hb, 1, 1)
    ring_in("p", pb, 3)
    keep_s = ring_start("s", st, sb)
    ring_mate("s", sb)
    weights_at(pb, rhs_p, 3)
    second_in("h", hb, 1, 2)
    ring_in("p", pb, 4)
    weights_at(pb, rhs_p, 4)
    product(hb, rhs_p, 0)
    give("dy", 0)
    second_far("h", hb, 1)
    product(hb, rhs_p, 1)
    give("dy", 1)

    masked(0)
    keep_s.wait()
    weights(sb, rhs_s, z)
    first_in("y", yb, 0)
    masked(1)
    ring_in("s", sb, 1)
    weights_at(sb, rhs_s, 1)
    second_in("y", yb, 0, 0)
    first_far("y", yb, 0)
    first_in("y", yb, 1)
    ring_in("s", sb, 2)
    weights_at(sb, rhs_s, 2)
    second_in("y", yb, 0, 3)
    second_in("y", yb, 0, 1)
    second_in("y", yb, 1, 0)
    first_far("y", yb, 1)
    ring_in("s", sb, 3)
    weights_at(sb, rhs_s, 3)
    second_in("y", yb, 0, 2)
    second_in("y", yb, 1, 3)
    second_in("y", yb, 1, 1)
    second_far("y", yb, 0)
    ring_in("s", sb, 4)
    weights_at(sb, rhs_s, 4)
    gifts[0].wait_send()
    product(yb, rhs_s, 0)
    give("dx", 0)
    second_in("y", yb, 1, 2)
    gifts[1].wait_send()

    def to_middle(g):
        return pltpu.make_async_remote_copy(
            src_ref=xs.at[g], dst_ref=im.at[g], send_sem=send_sem.at[POOL + 2 + g],
            recv_sem=recv_sem.at[NCOPY + g], device_id=middle, device_id_type=MESH,
        )

    def onward(g):
        return pltpu.make_async_remote_copy(
            src_ref=im.at[g], dst_ref=tr.at[own_place], send_sem=send_sem.at[POOL + 2 + 4 + g],
            recv_sem=recv_sem.at[NCOPY + 4 + own_place], device_id=final(g), device_id_type=MESH,
        )

    def stay(src, dst):
        copied = pltpu.make_async_copy(src, dst, local_sem.at[2])
        copied.start()
        copied.wait()

    def either(away, there, here_):
        pl.when(away)(there)
        pl.when(jnp.logical_not(away))(here_)

    def chunks_out(half):
        arrived(("dx", half), part.at[1, pl.ds(half * HALF, HALF)])
        for g in (2 * half, 2 * half + 1):
            for k in range(2):
                base = g * QUARTER + k * BS
                for odd in range(2):
                    strip = pl.ds(base + 32 * odd, 32)
                    value = acc[q, strip, :] + part[1, strip, :]
                    xt[strip, :] = value
                    xs[g, pl.ds(k * BS + odd, 32, 2), :] = value
            either(
                other(middle),
                lambda g=g: to_middle(g).start(),
                lambda g=g: stay(xs.at[g], im.at[g]),
            )

    def chunks_on(half):
        for g in (2 * half, 2 * half + 1):
            @pl.when(other(giver))
            def _(g=g):
                to_middle(g).wait_recv()

            either(
                other(final(g)),
                lambda g=g: onward(g).start(),
                lambda g=g: stay(im.at[g], tr.at[g]),
            )

    chunks_out(0)
    second_far("y", yb, 1)
    product(yb, rhs_s, 1)
    give("dx", 1)
    chunks_on(0)
    chunks_out(1)
    chunks_on(1)

    bl[CAP] = jnp.zeros((32, WIDTH), F32)
    for g in range(4):
        @pl.when(other(relay(g)))
        def _(g=g):
            pltpu.make_async_remote_copy(
                src_ref=tr.at[g], dst_ref=tr.at[g], send_sem=send_sem.at[POOL + 2 + 4 + g],
                recv_sem=recv_sem.at[NCOPY + 4 + g], device_id=partner, device_id_type=MESH,
            ).wait_recv()

        zt[...] = tr[g].T
        for k in range(2):
            i = 2 * g + k
            top = xt[pl.ds(i * BS, 32), :] + zt[pl.ds(k * BS, 32, 2), :]
            bottom = xt[pl.ds(i * BS + 32, 32), :] + zt[pl.ds(k * BS + 1, 32, 2), :]
            bl[2 * i] = jnp.where(low, top, pltpu.roll(bottom, BS, 1))
            bl[2 * i + 1] = jnp.where(low, pltpu.roll(top, BS, 1), bottom)

    @pl.loop(0, CAP)
    def _(slot):
        out_ref[slot] = bl[index_ref[4 * CAP + slot]]

    for g in range(4):
        @pl.when(other(middle))
        def _(g=g):
            to_middle(g).wait_send()

        @pl.when(other(final(g)))
        def _(g=g):
            onward(g).wait_send()

    assert len(used) == NCOPY, len(used)
    for made in started[-POOL:]:
        made.wait_send()


def shards(
    h_values, h_places, h_counts, p_values, p_places, p_counts,
    s_values, s_places, s_counts, x_places, x_counts,
):
    vmem = pl.BlockSpec(memory_space=pltpu.VMEM)
    anywhere = pl.BlockSpec(memory_space=pl.ANY)
    out = pl.pallas_call(
        kernel,
        out_shape=jax.ShapeDtypeStruct((CAP, 32, WIDTH), F32),
        in_specs=[anywhere] * 11,
        out_specs=vmem,
        scratch_shapes=[
            pltpu.SMEM((1, CAP), jnp.int32), pltpu.SMEM((1, 1), jnp.int32),
            pltpu.SMEM((1, CAP), jnp.int32), pltpu.SMEM((1, 1), jnp.int32),
            pltpu.SMEM((1, CAP), jnp.int32), pltpu.SMEM((1, 1), jnp.int32),
            pltpu.SMEM((1, CAP), jnp.int32), pltpu.SMEM((1, 1), jnp.int32),
            pltpu.SMEM((5 * CAP,), jnp.int32),
            pltpu.VMEM((3, 1, CAP, BS * BS), F32),
            pltpu.VMEM((CAP + 1, 32, WIDTH), F32),
            pltpu.VMEM((CAP + 1, 32, WIDTH), F32),
            pltpu.VMEM((CAP + 1, 32, WIDTH), F32),
            pltpu.VMEM((16, TILE, WIDTH), F32),
            pltpu.VMEM((16, TILE, WIDTH), F32),
            pltpu.VMEM((2, 2, 128, WIDTH), F32),
            pltpu.VMEM((2, 2, 128, WIDTH), F32),
            pltpu.VMEM((8, 2, 2, 128, WIDTH), F32),
            pltpu.VMEM((8, 2, 2, 128, WIDTH), F32),
            pltpu.VMEM((16, 384, 2 * WIDTH), BF16),
            pltpu.VMEM((16, 384, 2 * WIDTH), BF16),
            pltpu.VMEM((2, TILE, WIDTH), F32),
            pltpu.VMEM((2, TILE, WIDTH), F32),
            pltpu.VMEM((TILE, WIDTH), F32),
            pltpu.VMEM((4, 128, WIDTH), F32),
            pltpu.VMEM((4, 128, WIDTH), F32),
            pltpu.VMEM((128, WIDTH), F32),
            pltpu.VMEM((CAP + 1, 32, WIDTH), F32),
            pltpu.VMEM((4, 128, WIDTH), F32),
            pltpu.SemaphoreType.DMA((POOL + 10,)),
            pltpu.SemaphoreType.DMA((NCOPY + 8,)),
            pltpu.SemaphoreType.DMA((3,)),
            pltpu.SemaphoreType.DMA((11,)),
        ],
        compiler_params=pltpu.CompilerParams(
            collective_id=0, has_side_effects=True, vmem_limit_bytes=48 * 1024 * 1024
        ),
    )(
        h_places, h_counts, p_places, p_counts, s_places, s_counts, x_places, x_counts,
        h_values, p_values, s_values,
    )
    return out.reshape(1, CAP, BS * BS)


def solution(mesh):
    tile = P("row", "col", None)
    flat = P("row", "col")
    in_specs = (tile, flat, flat) * 3 + (flat, flat)
    return jax.shard_map(shards, mesh=mesh, in_specs=in_specs, out_specs=tile, check_vma=False)
```

```python
import jax
import jax.numpy as jnp
from jax import lax
from jax.experimental import pallas as pl
from jax.experimental.pallas import tpu as pltpu
from jax.sharding import PartitionSpec as P

MESH = pl.DeviceIdType.MESH
F32 = jnp.float32
BF16 = jnp.bfloat16
BS = 64
CAP = 16
TILE = 512
WIDTH = 128
HALF = 256
QUARTER = 128
NCOPY = 198
POOL = 48


def split(value):
    high = value.astype(BF16)
    return high, (value - high.astype(F32)).astype(BF16)


def kernel(
    hp_ref, hc_ref, pp_ref, pc_ref, sp_ref, sc_ref, xp_ref, xc_ref, h_ref, p_ref, s_ref, out_ref,
    hp, hc, pp, pc, sp, sc, xp, xc, index_ref, raw, hv, pv, sv, hb, yb, pt, st, pb, sb, rhs_p, rhs_s, acc, part, xt, xs, tr, zt, bl,
    im, send_sem, recv_sem, local_sem, load_sem,
):
    loads = [
        pltpu.make_async_copy(src, dst, load_sem.at[n])
        for n, (src, dst) in enumerate((
            (hp_ref, hp), (hc_ref, hc), (pp_ref, pp), (pc_ref, pc), (sp_ref, sp), (sc_ref, sc),
            (xp_ref, xp), (xc_ref, xc), (h_ref, raw.at[0]), (p_ref, raw.at[1]), (s_ref, raw.at[2]),
        ))
    ]
    for load in loads:
        load.start()
    z = lax.axis_index("row")
    col = lax.axis_index("col")
    q = lax.rem(col, 2)
    y = lax.rem(col // 2, 4)
    x = col // 8
    lane = lax.broadcasted_iota(jnp.int32, (32, WIDTH), 1)
    low = lane < BS

    def device(dz, dx, dy):
        return (
            lax.rem(z + dz, 8),
            lax.rem(x + dx, 4) * 8 + lax.rem(y + dy, 4) * 2 + q,
        )

    partner = (z, col + 1 - 2 * q)
    mirror_row = col // 4

    own_place = lax.rem(col, 4)

    panel = mirror_row
    middle = (z, 4 * lax.rem(z + panel, 8) + own_place)
    giver = (z, 4 * lax.rem(panel - z + 8, 8) + own_place)

    def final(g):
        return (lax.rem(panel - z + 8, 8), 4 * z + g)

    def relay(k):
        return (panel, 4 * lax.rem(z + panel, 8) + k)

    def other(device_id):
        return jnp.logical_or(device_id[0] != z, device_id[1] != col)

    barrier = pltpu.get_barrier_semaphore()
    for target in (
        device(0, 0, 1), device(0, 0, 3), device(0, 1, 0), device(0, 3, 0),
        device(1, 0, 0), device(7, 0, 0), partner,
    ):
        pl.semaphore_signal(barrier, inc=1, device_id=target, device_id_type=MESH)
    used, started, gifts = {}, [], []

    def copy(name, src, dst, target, sent=0):
        if name not in used:
            used[name] = len(used)
        return pltpu.make_async_remote_copy(
            src_ref=src, dst_ref=dst, send_sem=send_sem.at[sent], recv_sem=recv_sem.at[used[name]],
            device_id=target, device_id_type=MESH,
        )

    def send(name, src, dst, target, kept=None):
        if kept is None:
            if len(started) >= POOL:
                started[-POOL].wait_send()
            made = copy(name, src, dst, target, len(started) % POOL)
            started.append(made)
        else:
            made = copy(name, src, dst, target, POOL + len(kept))
            kept.append(made)
        made.start()

    def arrived(name, dst):
        copy(name, dst, dst, partner).wait_recv()

    def place_rows(values, base, dst, index):
        @pl.loop(0, 8)
        def _(i):
            a = values[index_ref[base + 2 * i]]
            b = values[index_ref[base + 2 * i + 1]]
            top = jnp.where(low, a, pltpu.roll(b, BS, 1))
            bottom = jnp.where(low, pltpu.roll(a, BS, 1), b)
            start = pl.multiple_of(i * BS, BS)
            dst[index, pl.ds(start, 32), :] = top
            dst[index, pl.ds(start + 32, 32), :] = bottom

    def place_natural(values, base, dst):
        for i in range(8):
            a = values[index_ref[base + 2 * i]]
            b = values[index_ref[base + 2 * i + 1]]
            even = jnp.where(low, a, pltpu.roll(b, BS, 1))
            odd = jnp.where(low, pltpu.roll(a, BS, 1), b)
            g = i // 2
            view = dst.at[g % 2, g // 2]
            view[pl.ds((i % 2) * BS, 32, 2), :] = even
            view[pl.ds((i % 2) * BS + 1, 32, 2), :] = odd

    for load in loads:
        load.wait()
    for m, (places, counts) in enumerate(((hp, hc), (pp, pc), (sp, sc), (xp, xc))):
        count = counts[0, 0]

        @pl.loop(0, CAP)
        def _(place, m=m, places=places, count=count):
            slot = CAP
            for k in range(CAP):
                slot = jnp.where(jnp.logical_and(places[0, k] == place, k < count), k, slot)
            index_ref[m * CAP + place] = slot

    @pl.loop(0, CAP)
    def _(slot):
        index_ref[4 * CAP + slot] = jnp.where(slot < xc[0, 0], xp[0, slot], CAP)

    for m, values in enumerate((hv, pv, sv)):
        values[pl.ds(0, CAP)] = raw[m, 0].reshape(CAP, 32, WIDTH)
        values[CAP] = jnp.zeros((32, WIDTH), F32)
    here = x * 4 + y
    place_rows(hv, 0, hb, here)
    place_natural(pv, CAP, pt)
    place_natural(sv, 2 * CAP, st)

    pl.semaphore_wait(barrier, 7)

    def tile_at(first, a, b):
        dy, dx = (a, b) if first == 1 else (b, a)
        return lax.rem(x + dx, 4) * 4 + lax.rem(y + dy, 4)

    def step(first, stage, by):
        along_y = (first == 1) == (stage == 1)
        return device(0, 0, by) if along_y else device(0, by, 0)

    def whole(buf, part, side, a, b):
        return buf.at[tile_at(1 - side, a, b), pl.ds(part * HALF + side * QUARTER, QUARTER)]

    def piece(buf, part, side, a, b, k):
        start = part * HALF + side * QUARTER + k * BS
        return buf.at[tile_at(1 - side, a, b), pl.ds(start, BS)]

    def second_out(tag, buf, part, side, a):
        src = whole(buf, part, side, a, 0)
        for by in (1, 3):
            send((tag, part, side, "s2", a, by), src, src, step(1 - side, 2, by))

    def out(tag, buf, part):
        for side in range(2):
            src = whole(buf, part, side, 0, 0)
            for by in (1, 3):
                send((tag, part, side, "s1", by), src, src, step(1 - side, 1, by))
        for side in range(2):
            second_out(tag, buf, part, side, 0)

    def first_in(tag, buf, part):
        for by, a, k in ((1, 3, 0), (3, 1, 1)):
            for side in range(2):
                arrived((tag, part, side, "s1", by), whole(buf, part, side, a, 0))
                src = piece(buf, part, side, a, 0, k)
                send((tag, part, side, "f1", by), src, src, step(1 - side, 1, by))
                second_out(tag, buf, part, side, a)

    def first_far(tag, buf, part):
        for side in range(2):
            for by, k in ((1, 0), (3, 1)):
                arrived((tag, part, side, "f1", by), piece(buf, part, side, 2, 0, k))
            second_out(tag, buf, part, side, 2)

    def second_in(tag, buf, part, a):
        for by, b, k in ((1, 3, 0), (3, 1, 1)):
            for side in range(2):
                arrived((tag, part, side, "s2", a, by), whole(buf, part, side, a, b))
                src = piece(buf, part, side, a, b, k)
                send((tag, part, side, "f2", a, by), src, src, step(1 - side, 2, by))

    def second_far(tag, buf, part):
        for a in (0, 3, 1, 2):
            for side in range(2):
                for by, k in ((1, 0), (3, 1)):
                    arrived((tag, part, side, "f2", a, by), piece(buf, part, side, a, 2, k))

    def ring_start(tag, own, buf):
        keep = pltpu.make_async_copy(own.at[q], buf.at[z, q], local_sem.at[0 if tag == "p" else 1])
        keep.start()
        send((tag, "mate"), own.at[1 - q], buf.at[z, q], partner)
        for by in (1, 7):
            send((tag, "own", by, 1), own.at[q], buf.at[z, q], device(by, 0, 0))
        return keep

    def ring_mate(tag, buf):
        arrived((tag, "mate"), buf.at[z, 1 - q])
        src = buf.at[z, 1 - q]
        for by in (1, 7):
            send((tag, "other", by, 1), src, src, device(by, 0, 0))

    def ring_in(tag, buf, d):
        for kind, core in (("own", q), ("other", 1 - q)):
            for by in (1, 7):
                away = lax.rem(z + (8 - by) * d, 8)
                if d < 4:
                    arrived((tag, kind, by, d), buf.at[away, core])
                if d < 3:
                    src = buf.at[away, core]
                    send((tag, kind, by, d + 1), src, src, device(by, 0, 0))
                elif d == 3:
                    src = buf.at[away, core, 0 if by == 1 else 1]
                    send((tag, kind, by, 4), src, src, device(by, 0, 0))
                else:
                    arrived((tag, kind, by, 4), buf.at[away, core, 0 if by == 1 else 1])

    def weights(buf, rhs, away):
        for g in range(2):
            wide = jnp.concatenate([buf[away, 0, g], buf[away, 1, g]], axis=1)
            high, rest = split(wide)
            t = 2 * away + g
            rhs[t, pl.ds(0, 128), :] = high
            rhs[t, pl.ds(128, 128), :] = high
            rhs[t, pl.ds(256, 128), :] = rest

    def weights_at(buf, rhs, d):
        @pl.loop(0, 2 if d < 4 else 1)
        def _(k):
            weights(buf, rhs, lax.rem(z + jnp.where(k == 0, d, 8 - d), 8))

    def product(buf, rhs, half):
        rows = pl.ds(half * HALF, HALF)
        acc[0, rows, :] = jnp.zeros((HALF, WIDTH), F32)
        acc[1, rows, :] = jnp.zeros((HALF, WIDTH), F32)

        @pl.loop(0, 2)
        def _(t):
            parts = []
            for k in range(8):
                high, rest = split(buf[8 * t + k, rows, :])
                parts += [high, rest, high]
            term = jnp.dot(
                jnp.concatenate(parts, axis=1),
                rhs[pl.ds(8 * t, 8)].reshape(8 * 384, 2 * WIDTH),
                preferred_element_type=F32,
            )
            acc[0, rows, :] += term[:, :WIDTH]
            acc[1, rows, :] += term[:, WIDTH:]

    def give(tag, half):
        rows = pl.ds(half * HALF, HALF)
        send((tag, half), acc.at[1 - q, rows], part.at[0 if tag == "dy" else 1, rows], partner,
             gifts if tag == "dy" else None)

    def masked(half):
        rows = pl.ds(half * HALF, HALF)
        arrived(("dy", half), part.at[0, rows])
        wide = lax.broadcasted_iota(jnp.int32, (BS, WIDTH), 1)
        for i in range(4 * half, 4 * half + 4):
            kept = jnp.where(wide < BS, index_ref[3 * CAP + 2 * i], index_ref[3 * CAP + 2 * i + 1]) < CAP
            strip = pl.ds(i * BS, BS)
            yb[here, strip, :] = jnp.where(kept, acc[q, strip, :] + part[0, strip, :], 0.0)
        out("y", yb, half)

    out("h", hb, 0)
    keep_p = ring_start("p", pt, pb)
    ring_mate("p", pb)
    first_in("h", hb, 0)
    out("h", hb, 1)
    keep_p.wait()
    weights(pb, rhs_p, z)
    second_in("h", hb, 0, 0)
    ring_in("p", pb, 1)
    first_far("h", hb, 0)
    first_in("h", hb, 1)
    weights_at(pb, rhs_p, 1)
    second_in("h", hb, 0, 3)
    second_in("h", hb, 0, 1)
    second_in("h", hb, 1, 0)
    ring_in("p", pb, 2)
    first_far("h", hb, 1)
    weights_at(pb, rhs_p, 2)
    second_in("h", hb, 0, 2)
    second_far("h", hb, 0)
    second_in("h", hb, 1, 3)
    second_in("h", hb, 1, 1)
    ring_in("p", pb, 3)
    keep_s = ring_start("s", st, sb)
    ring_mate("s", sb)
    weights_at(pb, rhs_p, 3)
    second_in("h", hb, 1, 2)
    ring_in("p", pb, 4)
    weights_at(pb, rhs_p, 4)
    product(hb, rhs_p, 0)
    give("dy", 0)
    second_far("h", hb, 1)
    product(hb, rhs_p, 1)
    give("dy", 1)

    masked(0)
    keep_s.wait()
    weights(sb, rhs_s, z)
    first_in("y", yb, 0)
    masked(1)
    ring_in("s", sb, 1)
    weights_at(sb, rhs_s, 1)
    second_in("y", yb, 0, 0)
    first_far("y", yb, 0)
    first_in("y", yb, 1)
    ring_in("s", sb, 2)
    weights_at(sb, rhs_s, 2)
    second_in("y", yb, 0, 3)
    second_in("y", yb, 0, 1)
    second_in("y", yb, 1, 0)
    first_far("y", yb, 1)
    ring_in("s", sb, 3)
    weights_at(sb, rhs_s, 3)
    second_in("y", yb, 0, 2)
    second_in("y", yb, 1, 3)
    second_in("y", yb, 1, 1)
    second_far("y", yb, 0)
    ring_in("s", sb, 4)
    weights_at(sb, rhs_s, 4)
    gifts[0].wait_send()
    product(yb, rhs_s, 0)
    give("dx", 0)
    second_in("y", yb, 1, 2)
    gifts[1].wait_send()

    def to_middle(g):
        return pltpu.make_async_remote_copy(
            src_ref=xs.at[g], dst_ref=im.at[g], send_sem=send_sem.at[POOL + 2 + g],
            recv_sem=recv_sem.at[NCOPY + g], device_id=middle, device_id_type=MESH,
        )

    def onward(g):
        return pltpu.make_async_remote_copy(
            src_ref=im.at[g], dst_ref=tr.at[own_place], send_sem=send_sem.at[POOL + 2 + 4 + g],
            recv_sem=recv_sem.at[NCOPY + 4 + own_place], device_id=final(g), device_id_type=MESH,
        )

    def stay(src, dst):
        copied = pltpu.make_async_copy(src, dst, local_sem.at[2])
        copied.start()
        copied.wait()

    def either(away, there, here_):
        pl.when(away)(there)
        pl.when(jnp.logical_not(away))(here_)

    def chunks_out(half):
        arrived(("dx", half), part.at[1, pl.ds(half * HALF, HALF)])
        for g in (2 * half, 2 * half + 1):
            for k in range(2):
                base = g * QUARTER + k * BS
                for odd in range(2):
                    strip = pl.ds(base + 32 * odd, 32)
                    value = acc[q, strip, :] + part[1, strip, :]
                    xt[strip, :] = value
                    xs[g, pl.ds(k * BS + odd, 32, 2), :] = value
            either(
                other(middle),
                lambda g=g: to_middle(g).start(),
                lambda g=g: stay(xs.at[g], im.at[g]),
            )

    def chunks_on(half):
        for g in (2 * half, 2 * half + 1):
            @pl.when(other(giver))
            def _(g=g):
                to_middle(g).wait_recv()

            either(
                other(final(g)),
                lambda g=g: onward(g).start(),
                lambda g=g: stay(im.at[g], tr.at[g]),
            )

    chunks_out(0)
    second_far("y", yb, 1)
    product(yb, rhs_s, 1)
    give("dx", 1)
    chunks_on(0)
    chunks_out(1)
    chunks_on(1)

    bl[CAP] = jnp.zeros((32, WIDTH), F32)
    for g in range(4):
        @pl.when(other(relay(g)))
        def _(g=g):
            pltpu.make_async_remote_copy(
                src_ref=tr.at[g], dst_ref=tr.at[g], send_sem=send_sem.at[POOL + 2 + 4 + g],
                recv_sem=recv_sem.at[NCOPY + 4 + g], device_id=partner, device_id_type=MESH,
            ).wait_recv()

        zt[...] = tr[g].T
        for k in range(2):
            i = 2 * g + k
            top = xt[pl.ds(i * BS, 32), :] + zt[pl.ds(k * BS, 32, 2), :]
            bottom = xt[pl.ds(i * BS + 32, 32), :] + zt[pl.ds(k * BS + 1, 32, 2), :]
            bl[2 * i] = jnp.where(low, top, pltpu.roll(bottom, BS, 1))
            bl[2 * i + 1] = jnp.where(low, pltpu.roll(top, BS, 1), bottom)

    @pl.loop(0, CAP)
    def _(slot):
        out_ref[slot] = bl[index_ref[4 * CAP + slot]]

    for g in range(4):
        @pl.when(other(middle))
        def _(g=g):
            to_middle(g).wait_send()

        @pl.when(other(final(g)))
        def _(g=g):
            onward(g).wait_send()

    assert len(used) == NCOPY, len(used)
    for made in started[-POOL:]:
        made.wait_send()


def shards(
    h_values, h_places, h_counts, p_values, p_places, p_counts,
    s_values, s_places, s_counts, x_places, x_counts,
):
    vmem = pl.BlockSpec(memory_space=pltpu.VMEM)
    anywhere = pl.BlockSpec(memory_space=pl.ANY)
    out = pl.pallas_call(
        kernel,
        out_shape=jax.ShapeDtypeStruct((CAP, 32, WIDTH), F32),
        in_specs=[anywhere] * 11,
        out_specs=vmem,
        scratch_shapes=[
            pltpu.SMEM((1, CAP), jnp.int32), pltpu.SMEM((1, 1), jnp.int32),
            pltpu.SMEM((1, CAP), jnp.int32), pltpu.SMEM((1, 1), jnp.int32),
            pltpu.SMEM((1, CAP), jnp.int32), pltpu.SMEM((1, 1), jnp.int32),
            pltpu.SMEM((1, CAP), jnp.int32), pltpu.SMEM((1, 1), jnp.int32),
            pltpu.SMEM((5 * CAP,), jnp.int32),
            pltpu.VMEM((3, 1, CAP, BS * BS), F32),
            pltpu.VMEM((CAP + 1, 32, WIDTH), F32),
            pltpu.VMEM((CAP + 1, 32, WIDTH), F32),
            pltpu.VMEM((CAP + 1, 32, WIDTH), F32),
            pltpu.VMEM((16, TILE, WIDTH), F32),
            pltpu.VMEM((16, TILE, WIDTH), F32),
            pltpu.VMEM((2, 2, 128, WIDTH), F32),
            pltpu.VMEM((2, 2, 128, WIDTH), F32),
            pltpu.VMEM((8, 2, 2, 128, WIDTH), F32),
            pltpu.VMEM((8, 2, 2, 128, WIDTH), F32),
            pltpu.VMEM((16, 384, 2 * WIDTH), BF16),
            pltpu.VMEM((16, 384, 2 * WIDTH), BF16),
            pltpu.VMEM((2, TILE, WIDTH), F32),
            pltpu.VMEM((2, TILE, WIDTH), F32),
            pltpu.VMEM((TILE, WIDTH), F32),
            pltpu.VMEM((4, 128, WIDTH), F32),
            pltpu.VMEM((4, 128, WIDTH), F32),
            pltpu.VMEM((128, WIDTH), F32),
            pltpu.VMEM((CAP + 1, 32, WIDTH), F32),
            pltpu.VMEM((4, 128, WIDTH), F32),
            pltpu.SemaphoreType.DMA((POOL + 10,)),
            pltpu.SemaphoreType.DMA((NCOPY + 8,)),
            pltpu.SemaphoreType.DMA((3,)),
            pltpu.SemaphoreType.DMA((11,)),
        ],
        compiler_params=pltpu.CompilerParams(
            collective_id=0, has_side_effects=True, vmem_limit_bytes=48 * 1024 * 1024
        ),
    )(
        h_places, h_counts, p_places, p_counts, s_places, s_counts, x_places, x_counts,
        h_values, p_values, s_values,
    )
    return out.reshape(1, CAP, BS * BS)


def solution(mesh):
    tile = P("row", "col", None)
    flat = P("row", "col")
    in_specs = (tile, flat, flat) * 3 + (flat, flat)
    return jax.shard_map(shards, mesh=mesh, in_specs=in_specs, out_specs=tile, check_vma=False)
```
